256 devices in a mesh: row: 16 (over x_hi, z), col: 16 (over y, x_lo, core).
Axes of the slice: x: 4 (x_hi: 2, x_lo: 2; x = x_hi * 2 + x_lo), y: 4, z: 8, core: 2. Of those that a mesh axis runs over, the one named last changes fastest.
Arguments:
- node_feats: bfloat16 [65536, 256], P(('row', 'col')), may hold values from -6 to 6
- dest_grad: bfloat16 [16, 4096, 256], P('col', 'row'), may hold values from -6 to 6
- bases: bfloat16 [30, 256, 256], replicated, may hold values from -0.375 to 0.375
- coefs: bfloat16 [2000, 30], replicated, may hold values from -1 to 1
- src_ids: int32 [16, 16, 1024], P('row', 'col'), may hold values from 0 to 4095
- dst_ids: int32 [16, 16, 1024], P('row', 'col'), may hold values from 0 to 4095
- rel_ids: int32 [16, 16, 1024], P('row', 'col'), may hold values from 0 to 1999
- edge_norm: float32 [16, 16, 1024], P('row', 'col'), may hold values from 0.1 to 1
- block_fill: int32 [16, 16, 8], P('row', 'col'), may hold values from 0 to 128, as said below
Outputs:
- node_grad: bfloat16 [65536, 256], P(('row', 'col'))
- basis_grad: float32 [7680, 256], P(('row', 'col'))
- coef_grad: float32 [2000, 30], replicated
The draws below stay inside these ranges and needn't reach their ends.
Inputs may be any that keep to these rules, and one draw needn't show every extreme that they name: `block_fill`: the first block of every device is full, and blocks after a device's last live block are empty.
All inputs are finite; a program needn't handle non-finite values.
Results may differ from the reference program's by a relative error of at most 0.0049.
Values may be sent and summed in bfloat16 or wider, within the bound.
A program may use at most 64 MiB of HBM per device.

```python
import math
import jax
import jax.numpy as jnp
from jax import lax

D = 256
BASES = 30
RELS = 2000
VS = 256
EBLK = 8
EDGE_BLOCK = 128
EDEV = 1024
VERTS = 65536
N_ROW = 16
N_COL = 16


def draw_block_fill(key, part):
    first_key = jax.random.fold_in(key, 11)
    second_key = jax.random.fold_in(key, 23)
    live_blocks = jax.random.randint(first_key, (N_ROW, N_COL, 1), 1, EBLK + 1)
    fills = jax.random.randint(second_key, (N_ROW, N_COL, EBLK), 1, EDGE_BLOCK + 1)
    index = jnp.arange(EBLK, dtype=jnp.int32)[None, None, :]
    fills = jnp.where(index == 0, EDGE_BLOCK, fills)
    return jnp.where(index < live_blocks, fills, 0).astype(jnp.int32)


def plant(entries, own_key, least, largest):
    dims = entries.shape
    place = [jax.random.randint(jax.random.fold_in(own_key, axis), (), 0, dims[axis]) for axis in range(len(dims))]
    entries = entries.at[tuple(place)].set(least)
    longest = dims.index(max(dims))
    place[longest] = (place[longest] + 1) % dims[longest]
    return entries.at[tuple(place)].set(largest)


def level_of(rng, shape, cuts, least, top_value):
    gain = 1.0
    for dim, blocks in cuts:
        heights = jax.random.uniform(jax.random.fold_in(jax.random.fold_in(rng, 6), dim), (blocks,), jnp.float32, least / len(cuts), top_value / len(cuts))
        gain = gain * jnp.repeat(jnp.exp(heights), shape[dim] // blocks).reshape((-1,) + (1,) * (len(shape) - 1 - dim))
    return gain


def centred(rng, extent, scale, bound, split=(), held_as=jnp.bfloat16):
    array = scale * jax.random.normal(rng, extent, jnp.float32)
    if split:
        array = array * level_of(rng, extent, split, -0.22, 0.18)
    return jnp.clip(array, -bound, bound).astype(held_as)


def setup_inputs(seed: int = 0) -> dict:
    streams_of = jax.random.split(jax.random.key(seed), 10)
    node_feats = centred(streams_of[0], (VERTS, D), 1.0, 6.0, ((0, 256),))
    dest_grad = centred(streams_of[1], (N_COL, N_ROW * VS, D), 1.0, 6.0, ((0, 16), (1, 16)))
    bases = centred(streams_of[2], (BASES, D, D), D ** -0.5, 0.375)
    coefs = centred(streams_of[3], (RELS, BASES), BASES ** -0.5, 1.0)
    src_ids = plant(jax.random.randint(streams_of[4], (N_ROW, N_COL, EDEV), 0, VS * N_COL), jax.random.fold_in(streams_of[4], 1), 0, (VS * N_COL) - 1).astype(jnp.int32)
    dst_ids = plant(jax.random.randint(streams_of[5], (N_ROW, N_COL, EDEV), 0, VS * N_ROW), jax.random.fold_in(streams_of[5], 1), 0, (VS * N_ROW) - 1).astype(jnp.int32)
    rel_ids = plant(jax.random.randint(streams_of[6], (N_ROW, N_COL, EDEV), 0, RELS), jax.random.fold_in(streams_of[6], 1), 0, RELS - 1).astype(jnp.int32)
    edge_norm = jnp.clip(jnp.exp(math.log(1.0) - 2.3025851 * jax.random.uniform(streams_of[7], (N_ROW, N_COL, EDEV), jnp.float32) ** level_of(streams_of[7], (N_ROW, N_COL, EDEV), ((0, 16), (1, 16)), -0.2, 0.2)), 0.1, 1.0)
    block_fill = draw_block_fill(jax.random.fold_in(streams_of[9], 71), 0)
    return dict(node_feats=node_feats, dest_grad=dest_grad, bases=bases, coefs=coefs, src_ids=src_ids, dst_ids=dst_ids, rel_ids=rel_ids, edge_norm=edge_norm, block_fill=block_fill)


def reference(node_feats, dest_grad, bases, coefs, src_ids, dst_ids, rel_ids, edge_norm, block_fill):
    verts = node_feats.shape[0]
    width = node_feats.shape[1]
    targets_all = dest_grad.reshape(verts, width)
    slot = jnp.arange(EDEV, dtype=jnp.int32)
    position = slot % EDGE_BLOCK
    which = slot // EDGE_BLOCK
    fills = jnp.take(block_fill, which, axis=2)
    live_mask = (position[None, None, :] < fills).astype(jnp.float32)
    weights = (edge_norm * live_mask).reshape(-1, EDEV)
    row_base = (jnp.arange(N_ROW, dtype=jnp.int32) * (VS * N_COL))[:, None, None]
    col_base = (jnp.arange(N_COL, dtype=jnp.int32) * (VS * N_ROW))[None, :, None]
    sources = (src_ids + row_base).astype(jnp.int32).reshape(-1, EDEV)
    targets = (dst_ids + col_base).astype(jnp.int32).reshape(-1, EDEV)
    relations = rel_ids.reshape(-1, EDEV)
    bases_wide = bases.astype(jnp.float32)

    def step(carry, block):
        node_part, coef_part, basis_part = carry
        weight, source, target, relation = block
        edge_grad = (weight[:, None] * targets_all[target].astype(jnp.float32)).astype(jnp.bfloat16)
        edge_rows = node_feats[source]
        edge_coefs = coefs[relation].astype(jnp.float32)
        backed = jnp.einsum('em,bkm->ebk', edge_grad.astype(jnp.float32), bases_wide)
        per_edge = jnp.sum(edge_coefs[:, :, None] * backed, axis=1)
        inner = jnp.sum(backed * edge_rows.astype(jnp.float32)[:, None, :], axis=2)
        basis_rows = (edge_coefs[:, :, None] * edge_rows.astype(jnp.float32)[:, None, :]).reshape(EDEV, BASES * D).astype(jnp.bfloat16)
        node_part = node_part + jax.ops.segment_sum(per_edge, source, num_segments=verts)
        coef_part = coef_part + jax.ops.segment_sum(inner, relation, num_segments=RELS)
        basis_part = basis_part + jnp.dot(basis_rows.T, edge_grad, preferred_element_type=jnp.float32)
        return (node_part, coef_part, basis_part), None

    start = (jnp.zeros((verts, width), jnp.float32), jnp.zeros((RELS, BASES), jnp.float32), jnp.zeros((BASES * D, D), jnp.float32))
    (node_part, coef_part, basis_part), _ = lax.scan(step, start, (weights, sources, targets, relations))
    return node_part.astype(jnp.bfloat16), basis_part / N_COL, coef_part / N_COL
```

```python
import functools

import jax
import jax.numpy as jnp
from jax import lax
from jax.experimental import pallas as pl
from jax.experimental.pallas import tpu as pltpu
from jax.sharding import PartitionSpec as P

MESH = pl.DeviceIdType.MESH
BF16 = jnp.bfloat16
F32 = jnp.float32
D = 256
BASES = 30
RELS = 2000
EDGES = 1024
EDGE_BLOCK = 128
VMEM = pltpu.VMEM


class Place:
    def __init__(self):
        i, j = lax.axis_index("row"), lax.axis_index("col")
        self.i, self.j = i, j
        self.z, self.xh = lax.rem(i, 8), lax.div(i, 8)
        self.y, self.xl, self.c = lax.div(j, 4), lax.rem(lax.div(j, 2), 2), lax.rem(j, 2)
        self.x = self.xh * 2 + self.xl

    def at(self, z=None, y=None, x=None, c=None):
        z = self.z if z is None else z
        y = self.y if y is None else y
        x = self.x if x is None else x
        c = self.c if c is None else c
        return (lax.div(x, 2) * 8 + z, y * 4 + lax.rem(x, 2) * 2 + c)


def wrap(value, n):
    return lax.rem(value + 2 * n, n)


def greet(peers):
    barrier = pltpu.get_barrier_semaphore()
    for peer in peers:
        pl.semaphore_signal(barrier, inc=1, device_id=peer, device_id_type=MESH)
    pl.semaphore_wait(barrier, len(peers))


class Mail:
    def __init__(self, send_sems, recv_sems):
        self.send_sems, self.recv_sems, self.count, self.sent = send_sems, recv_sems, 0, []

    def send(self, src, dst, peer):
        copy = pltpu.make_async_remote_copy(
            src_ref=src,
            dst_ref=dst,
            send_sem=self.send_sems.at[self.count],
            recv_sem=self.recv_sems.at[self.count],
            device_id=peer,
            device_id_type=MESH,
        )
        self.count += 1
        copy.start()
        self.sent.append(copy)
        return copy

    def finish(self):
        for copy in self.sent:
            copy.wait_send()


GATHER_MESSAGES = 40


def gather_kernel(
    fill, nf, dg, src, dst, rel, norm, coefs, xt_out, gt_out, ct_out,
    nbuf, dbuf, xacc, gacc, send_sems, recv_sems,
):
    me = Place()
    mail = Mail(send_sems, recv_sems)
    zup, zdn = me.at(z=wrap(me.z + 1, 8)), me.at(z=wrap(me.z - 1, 8))
    yup, ydn = me.at(y=wrap(me.y + 1, 4)), me.at(y=wrap(me.y - 1, 4))
    xnear = me.at(x=me.xh * 2 + 1 - me.xl)
    xfar = me.at(x=(1 - me.xh) * 2 + me.xl)
    sib = me.at(c=1 - me.c)
    greet([zup, zdn, yup, ydn, xnear, xfar, sib])

    def drow(q, z):
        return (me.xh if q == 0 else 1 - me.xh) * 8 + wrap(z, 8)

    def ncol(q, y, c):
        return wrap(y, 4) * 4 + (me.xl if q == 0 else 1 - me.xl) * 2 + c

    def dsend(q, d, up):
        sign = -1 if up else 1
        slot = drow(q, me.z + sign * d)
        peer = zup if up else zdn
        if d == 0 and q == 0:
            return mail.send(dg, dbuf.at[slot], peer)
        if d < 3:
            return mail.send(dbuf.at[slot], dbuf.at[slot], peer)
        half = pl.ds(0, 128) if up else pl.ds(128, 128)
        return mail.send(dbuf.at[slot, half], dbuf.at[slot, half], peer)

    def nsend(q, d, up):
        sign = -1 if up else 1
        slot = ncol(q, me.y + sign * d, me.c)
        peer = yup if up else ydn
        if d == 0 and q == 0:
            return mail.send(nf, nbuf.at[slot], peer)
        if d == 0:
            return mail.send(nbuf.at[slot], nbuf.at[slot], peer)
        half = pl.ds(0, 128) if up else pl.ds(128, 128)
        return mail.send(nbuf.at[slot, half], nbuf.at[slot, half], peer)

    def pass_on(slot):
        return mail.send(nbuf.at[slot], nbuf.at[slot], sib)

    vertex = lax.broadcasted_iota(jnp.int32, (256, EDGES), 0)

    def select(ids, base, rows, acc, first=False):
        hot = jnp.where(vertex + base == ids[...], 1.0, 0.0).astype(BF16)
        picked = lax.dot_general(
            rows, hot, (((0,), (0,)), ((), ())), preferred_element_type=F32
        )
        if first:
            acc[...] = picked
        else:
            acc[...] += picked

    def take_d(slot):
        select(dst, slot * 256, dbuf[slot], gacc)

    def take_n(slot):
        select(src, slot * 256, nbuf[slot], xacc)

    d = {}
    n = {}
    d[0, 0, 1], d[0, 0, 0] = dsend(0, 0, True), dsend(0, 0, False)
    far = mail.send(dg, dbuf.at[drow(0, me.z)], xfar)
    near = mail.send(nf, nbuf.at[ncol(0, me.y, me.c)], xnear)
    n[0, 0, 1], n[0, 0, 0] = nsend(0, 0, True), nsend(0, 0, False)
    own = mail.send(nf, nbuf.at[ncol(0, me.y, me.c)], sib)

    select(dst, me.i * 256, dg[...], gacc, first=True)
    select(src, me.j * 256, nf[...], xacc, first=True)

    for up in (1, 0):
        d[0, 0, up].wait_recv()
        d[0, 1, up] = dsend(0, 1, bool(up))
    far.wait_recv()
    for up in (1, 0):
        d[1, 0, up] = dsend(1, 0, bool(up))
    near.wait_recv()
    for up in (1, 0):
        n[1, 0, up] = nsend(1, 0, bool(up))
    passed = {(1, 0): pass_on(ncol(1, me.y, me.c))}
    for up in (1, 0):
        n[0, 0, up].wait_recv()
        n[0, 1, up] = nsend(0, 1, bool(up))
        passed[0, up] = pass_on(ncol(0, me.y + (-1 if up else 1), me.c))

    for start in range(0, RELS, 256):
        size = min(256, RELS - start)
        relation = lax.broadcasted_iota(jnp.int32, (size, EDGES), 0) + start
        hot = jnp.where(relation == rel[...], 1.0, 0.0).astype(BF16)
        part = lax.dot_general(
            coefs[start : start + size, :], hot, (((0,), (0,)), ((), ())),
            preferred_element_type=F32,
        )
        if start == 0:
            ct_out[0:BASES, :] = part
        else:
            ct_out[0:BASES, :] += part
    ct_out[BASES:32, :] = jnp.zeros((2, EDGES), F32)

    def arrive_d(q, dist, forward):
        for up in (1, 0):
            d[q, dist, up].wait_recv()
            if forward:
                d[q, dist + 1, up] = dsend(q, dist + 1, bool(up))

    def both_d(q, dist):
        take_d(drow(q, me.z - dist))
        take_d(drow(q, me.z + dist))

    arrive_d(0, 1, True)
    both_d(0, 1)
    take_d(drow(1, me.z))
    take_n(ncol(1, me.y, me.c))
    arrive_d(1, 0, True)
    for up in (1, 0):
        n[1, 0, up].wait_recv()
        n[1, 1, up] = nsend(1, 1, bool(up))
        passed[1, 2 + up] = pass_on(ncol(1, me.y + (-1 if up else 1), me.c))
    own.wait_recv()
    take_n(ncol(0, me.y - 1, me.c))
    take_n(ncol(0, me.y + 1, me.c))
    take_n(ncol(0, me.y, 1 - me.c))
    both_d(1, 1)
    arrive_d(0, 2, True)
    for up in (1, 0):
        n[0, 1, up].wait_recv()
    passed[0, 2] = pass_on(ncol(0, me.y + 2, me.c))
    both_d(0, 2)
    take_n(ncol(0, me.y + 2, me.c))
    take_n(ncol(1, me.y + 1, me.c))
    take_n(ncol(1, me.y - 1, me.c))
    arrive_d(1, 1, True)
    for up in (1, 0):
        n[1, 1, up].wait_recv()
    passed[1, 4] = pass_on(ncol(1, me.y + 2, me.c))
    take_n(ncol(1, me.y + 2, me.c))
    for key in passed:
        passed[key].wait_recv()
    for q, y in ((1, me.y), (0, me.y - 1), (0, me.y + 1), (1, me.y - 1), (1, me.y + 1), (0, me.y + 2), (1, me.y + 2)):
        take_n(ncol(q, y, 1 - me.c))
    xt_out[...] = xacc[...].astype(BF16)
    arrive_d(0, 3, False)
    both_d(0, 3)
    take_d(drow(0, me.z + 4))
    arrive_d(1, 2, True)
    both_d(1, 2)
    both_d(1, 3)
    arrive_d(1, 3, False)
    take_d(drow(1, me.z + 4))

    lane = lax.broadcasted_iota(jnp.int32, (1, EDGE_BLOCK), 1)
    for block in range(EDGES // EDGE_BLOCK):
        lanes = pl.ds(block * EDGE_BLOCK, EDGE_BLOCK)
        weight = norm[:, lanes] * jnp.where(lane < fill[0, block], 1.0, 0.0).astype(F32)
        gt_out[:, lanes] = (gacc[:, lanes] * weight).astype(BF16)
    mail.finish()


def compute_kernel(
    xt, gt, ct, src, rel, bases, npart, bpart, grads, xf, per_edge, inner, coef_part, basis_part
):
    grads[...] = gt[...].T
    xf[...] = xt[...].astype(F32)
    per_edge[...] = jnp.zeros_like(per_edge)
    inner[BASES:32, :] = jnp.zeros((2, EDGES), F32)

    @pl.loop(0, BASES)
    def _(b):
        coef = ct[pl.ds(b, 1), :]
        backed = jnp.dot(bases[b], gt[...], preferred_element_type=F32)
        per_edge[...] += coef * backed
        inner[pl.ds(b, 1), :] = jnp.sum(backed * xf[...], axis=0, keepdims=True)
        scaled = (coef * xf[...]).astype(BF16)
        start = pl.multiple_of(b * D, D)
        basis_part[pl.ds(start, D), :] = jnp.dot(scaled, grads[...], preferred_element_type=F32)

    values = per_edge[...].T.astype(BF16)
    vertex = lax.broadcasted_iota(jnp.int32, (256, EDGES), 0)

    @pl.loop(0, 16)
    def _(block):
        hot = jnp.where(vertex + block * 256 == src[...], 1.0, 0.0).astype(BF16)
        slot = lax.rem(block, 2) * 8 + lax.div(block, 2)
        npart[slot] = jnp.dot(hot, values, preferred_element_type=F32).astype(BF16)

    high = inner[...].astype(BF16)
    low = (inner[...] - high.astype(F32)).astype(BF16)
    both = jnp.concatenate([high, low], axis=0)
    for block in range(8):
        hot = jnp.where(vertex + block * 256 == rel[...], 1.0, 0.0).astype(BF16)
        part = lax.dot_general(both, hot, (((1,), (1,)), ((), ())), preferred_element_type=F32)
        coef_part[:, block, :] = part[0:32] + part[32:64]

    @pl.loop(0, 32)
    def _(group):
        rows = basis_part[pl.ds(pl.multiple_of(group * 240, 8), 240), :]
        extra = coef_part[group]
        row = lax.div(group, 2)
        z, xh = lax.rem(row, 8), lax.div(row, 8)
        for u in range(8):
            y = lax.rem(2 * group + u // 4, 4)
            xl, c = (u % 4) // 2, u % 2
            slot = c * 128 + z * 16 + y * 4 + xh * 2 + xl
            piece = jnp.concatenate(
                [rows[30 * u : 30 * u + 30], extra[u : u + 1], jnp.zeros((1, D), F32)], axis=0
            ).astype(BF16)
            bpart[2 * slot] = piece[0:16]
            bpart[2 * slot + 1] = piece[16:32]


def ring_steps(mail, acc, base, unit, n, p, up, down, heads, bodies):
    half = unit // 2
    start = lambda q: base + wrap(q, n) * unit
    opposite = start(p + n // 2)
    flights = [
        mail.send(acc.at[pl.ds(opposite, half)], heads.at[0], up),
        mail.send(acc.at[pl.ds(opposite + half, half)], heads.at[1], down),
    ]
    for step in range(1, n // 2):
        following = []
        for way, peer in ((0, up), (1, down)):
            first = start(p + (n // 2 - step) * (1 if way == 0 else -1))
            yield
            flights[way].wait_recv()
            if step == 1:
                add_into(acc, first + way * half, half, [heads.at[way]])
            else:
                add_into(acc, first, unit, [bodies.at[way, step - 2]])
            following.append(mail.send(acc.at[pl.ds(first, unit)], bodies.at[way, step - 1], peer))
        flights = following
    yield
    for flight in flights:
        flight.wait_recv()
    last = n // 2 - 2
    add_into(acc, start(p), unit, [bodies.at[0, last], bodies.at[1, last]])


def add_into(acc, first, count, sources):
    def body(k, carry):
        total = acc[first + k].astype(F32)
        for source in sources:
            total = total + source[k].astype(F32)
        acc[first + k] = total.astype(BF16)
        return carry

    if count == 1:
        body(0, 0)
    else:
        lax.fori_loop(0, count, body, 0)


def run(*streams):
    streams = list(streams)
    while streams:
        for stream in list(streams):
            try:
                next(stream)
            except StopIteration:
                streams.remove(stream)


REDUCE_MESSAGES = 70


def reduce_kernel(
    npart, bpart, node_out, basis_out, coef_out,
    nfrom, nacc, nheads, nbodies, nnear, bfrom, bacc, zheads, zbodies, yheads, ybodies, xheads, xbodies,
    send_sems, recv_sems,
):
    me = Place()
    mail = Mail(send_sems, recv_sems)
    zup, zdn = me.at(z=wrap(me.z + 1, 8)), me.at(z=wrap(me.z - 1, 8))
    yup, ydn = me.at(y=wrap(me.y + 1, 4)), me.at(y=wrap(me.y - 1, 4))
    xup, xdn = me.at(x=wrap(me.x + 1, 4)), me.at(x=wrap(me.x - 1, 4))
    xnear = me.at(x=me.xh * 2 + 1 - me.xl)
    sib = me.at(c=1 - me.c)
    row_peers = [(wrap(me.i + k, 16), me.j) for k in range(1, 16)]
    col_peers = [(me.i, wrap(me.j + k, 16)) for k in range(1, 16)]
    greet(row_peers + col_peers + [xup, xdn])

    node_core = mail.send(npart.at[pl.ds((1 - me.c) * 8, 8)], nfrom, sib)
    basis_core = mail.send(bpart.at[pl.ds((1 - me.c) * 256, 256)], bfrom, sib)

    def node_stream():
        node_core.wait_recv()

        def body(k, carry):
            nacc[k] = (npart[me.c * 8 + k].astype(F32) + nfrom[k].astype(F32)).astype(BF16)
            return carry

        lax.fori_loop(0, 8, body, 0)
        yield from ring_steps(mail, nacc, 0, 2, 4, me.y, yup, ydn, nheads, nbodies)
        near = mail.send(nacc.at[me.y * 2 + 1 - me.xl], nnear, xnear)
        yield
        near.wait_recv()
        node_out[...] = (nacc[me.y * 2 + me.xl].astype(F32) + nnear[...].astype(F32)).astype(BF16)

    def basis_stream():
        basis_core.wait_recv()

        def body(k, carry):
            bacc[k] = (bpart[me.c * 256 + k].astype(F32) + bfrom[k].astype(F32)).astype(BF16)
            return carry

        lax.fori_loop(0, 256, body, 0)
        yield from ring_steps(mail, bacc, 0, 32, 8, me.z, zup, zdn, zheads, zbodies)
        base = me.z * 32
        yield from ring_steps(mail, bacc, base, 8, 4, me.y, yup, ydn, yheads, ybodies)
        base = base + me.y * 8
        yield from ring_steps(mail, bacc, base, 2, 4, me.x, xup, xdn, xheads, xbodies)
        base = base + me.x * 2
        total = jnp.concatenate([bacc[base].astype(F32), bacc[base + 1].astype(F32)], axis=0) * (1.0 / 16)
        basis_out[...] = total[0:BASES]
        mine = me.i * 16 + me.j
        coef_out[mine] = total[BASES : BASES + 1]
        flights = [mail.send(coef_out.at[mine], coef_out.at[mine], peer) for peer in col_peers]
        yield
        for flight in flights:
            flight.wait_recv()
        group = pl.ds(me.i * 16, 16)
        flights = [mail.send(coef_out.at[group], coef_out.at[group], peer) for peer in row_peers]
        yield
        for flight in flights:
            flight.wait_recv()

    run(node_stream(), basis_stream())
    mail.finish()


def on_device(
    node_feats, dest_grad, bases, coefs, src_ids, dst_ids, rel_ids, edge_norm, block_fill
):
    src, dst, rel = (a.reshape(1, EDGES) for a in (src_ids, dst_ids, rel_ids))
    norm = edge_norm.reshape(1, EDGES)
    vm = pl.BlockSpec(memory_space=VMEM)
    xt, gt, ct = pl.pallas_call(
        gather_kernel,
        out_shape=(
            jax.ShapeDtypeStruct((D, EDGES), BF16),
            jax.ShapeDtypeStruct((D, EDGES), BF16),
            jax.ShapeDtypeStruct((32, EDGES), F32),
        ),
        in_specs=[pl.BlockSpec(memory_space=pltpu.SMEM)] + [vm] * 7,
        out_specs=(vm, vm, vm),
        scratch_shapes=[
            VMEM((16, 256, D), BF16),
            VMEM((16, 256, D), BF16),
            VMEM((D, EDGES), F32),
            VMEM((D, EDGES), F32),
            pltpu.SemaphoreType.DMA((GATHER_MESSAGES,)),
            pltpu.SemaphoreType.DMA((GATHER_MESSAGES,)),
        ],
        compiler_params=pltpu.CompilerParams(collective_id=0, has_side_effects=True),
    )(block_fill.reshape(1, 8), node_feats, dest_grad[0], src, dst, rel, norm, coefs)
    npart, bpart = pl.pallas_call(
        compute_kernel,
        out_shape=(
            jax.ShapeDtypeStruct((16, 256, D), BF16),
            jax.ShapeDtypeStruct((512, 16, D), BF16),
        ),
        in_specs=[vm] * 6,
        out_specs=(vm, vm),
        scratch_shapes=[
            VMEM((EDGES, D), BF16),
            VMEM((D, EDGES), F32),
            VMEM((D, EDGES), F32),
            VMEM((32, EDGES), F32),
            VMEM((32, 8, D), F32),
            VMEM((BASES * D, D), F32),
        ],
    )(xt, gt, ct, src, rel, bases)
    dma = pltpu.SemaphoreType.DMA((REDUCE_MESSAGES,))
    node_grad, basis_grad, coef_rows = pl.pallas_call(
        reduce_kernel,
        out_shape=(
            jax.ShapeDtypeStruct((256, D), BF16),
            jax.ShapeDtypeStruct((BASES, D), F32),
            jax.ShapeDtypeStruct((256, 1, D), F32),
        ),
        in_specs=[vm] * 2,
        out_specs=(vm, vm, vm),
        scratch_shapes=[
            VMEM((8, 256, D), BF16),
            VMEM((8, 256, D), BF16),
            VMEM((2, 1, 256, D), BF16),
            VMEM((2, 1, 2, 256, D), BF16),
            VMEM((256, D), BF16),
            VMEM((256, 16, D), BF16),
            VMEM((256, 16, D), BF16),
            VMEM((2, 16, 16, D), BF16),
            VMEM((2, 3, 32, 16, D), BF16),
            VMEM((2, 4, 16, D), BF16),
            VMEM((2, 1, 8, 16, D), BF16),
            VMEM((2, 1, 16, D), BF16),
            VMEM((2, 1, 2, 16, D), BF16),
            dma,
            dma,
        ],
        compiler_params=pltpu.CompilerParams(collective_id=1, has_side_effects=True),
    )(npart, bpart)
    coef_grad = coef_rows.reshape(32, 2048)[:BASES, :RELS].T
    return node_grad, basis_grad, coef_grad


def solution(mesh):
    in_specs = (
        P(("row", "col"), None),
        P("col", "row", None),
        P(),
        P(),
        P("row", "col", None),
        P("row", "col", None),
        P("row", "col", None),
        P("row", "col", None),
        P("row", "col", None),
    )
    out_specs = (P(("row", "col"), None), P(("row", "col"), None), P())
    return jax.shard_map(
        on_device, mesh=mesh, in_specs=in_specs, out_specs=out_specs, check_vma=False
    )
```
